32 devices in a mesh: groups: 2 (over x), tile: 8 (over z, y), dp: 2 (over core).
Axes of the slice: x: 2, y: 2, z: 4, core: 2. Of those that a mesh axis runs over, the one named last changes fastest.
Arguments:
- activations: bfloat16 [4096, 8192], P(('groups', 'dp'), 'tile'), parts along dimension 0, may hold values from -6 to 6
- grads: bfloat16 [4096, 8192], P(('groups', 'dp'), 'tile'), parts along dimension 0
- group_index: int32 [16384], P(('groups', 'tile')), parts along dimension 0, may hold values from 0 to 3
- tile_list: int32 [128, 2], P('tile'), may hold values from -1 to 31, as said below
Outputs:
- hessians: float32 [256, 256, 4, 256], P('dp', ('groups', 'tile')), parts along dimension 1
The draws below stay inside these ranges and needn't reach their ends.
There are 2 independent parts, one for each index of `groups`. The reference program is written for one: setup_inputs(seed, part) draws one part's arguments, and reference() takes and returns one part's arrays. A program takes and returns all parts, laid end to end along the dimension named above; an argument that names none is the same for every part. Nothing has to cross between parts.
Inputs may be any that keep to these rules, and one draw needn't show every extreme that they name: `tile_list`: each index of tile holds 16 consecutive slots; its live slots (i >= 0) come first, at most 16 of them, and one index holds exactly 16. Live slots name distinct tiles with i <= j, 64 of them in all; empty slots hold -1 in both columns.
All inputs are finite; a program needn't handle non-finite values.
Results may differ from the reference program's by a relative error of at most 0.0024.
Values may be sent and summed in bfloat16 or wider, within the bound.
No kernel may reach another device: no remote copies, remote signals or barrier semaphores. Data moves between devices by JAX's collectives and lax.ppermute only.
A program may use at most 192 MiB of HBM per device.

```python
import jax
import jax.numpy as jnp
import numpy as np
from jax import lax

DIN = 8192
DOUT = 8192
GROUPS = 4
TILE = 256
MAXT = 16
ROWS = 2048
NB = 32
LIVE = 64
N_TILE = 8


def draw_grads(key, part):
    first, second, third = jax.random.split(key, 3)
    channel = jnp.arange(DOUT, dtype=jnp.float32) / DOUT
    rough = jax.random.uniform(second, (1, DOUT), jnp.float32, 0.5, 1.5)
    row_scale = jnp.exp(jax.random.uniform(third, (ROWS, 1), jnp.float32, jnp.log(0.5), jnp.log(2.0)))
    base = jnp.clip(jax.random.normal(first, (ROWS, DOUT), jnp.float32), -5.0, 5.0)
    values = base * (3.0 ** channel)[None, :] * rough * row_scale
    return values.astype(jnp.bfloat16)


def draw_tile_list(key, part):
    keys = jax.random.split(jax.random.fold_in(key, 17), 4)
    upper = np.triu_indices(NB)
    upper_rows = jnp.asarray(upper[0], dtype=jnp.int32)
    upper_cols = jnp.asarray(upper[1], dtype=jnp.int32)
    chosen = jax.random.permutation(keys[0], NB * (NB + 1) // 2)[:LIVE].astype(jnp.int32)
    pair_count = jax.random.randint(keys[1], (N_TILE // 2,), 0, MAXT + 1)
    pair_count = pair_count.at[0].set(MAXT)
    flip = jax.random.randint(keys[2], (N_TILE // 2,), 0, 2)
    first_count = jnp.where(flip == 1, pair_count, MAXT - pair_count)
    counts = jnp.stack([first_count, MAXT - first_count], 1).reshape(N_TILE)
    counts = counts[jax.random.permutation(keys[3], N_TILE)].astype(jnp.int32)
    offsets = jnp.cumsum(counts) - counts
    position = jnp.arange(MAXT, dtype=jnp.int32)[None, :]
    live = position < counts[:, None]
    index = jnp.minimum(offsets[:, None] + position, LIVE - 1)
    tile_id = chosen[index]
    rows = jnp.where(live, upper_rows[tile_id], -1)
    cols = jnp.where(live, upper_cols[tile_id], -1)
    return jnp.stack([rows, cols], -1).reshape(N_TILE * MAXT, 2).astype(jnp.int32)


def touch_ends(array, key, low, high):
    longest = array.shape.index(max(array.shape))
    spots = []
    for shift in (0, 1):
        where = [jax.random.randint(jax.random.fold_in(key, axis), (), 0, length) for axis, length in enumerate(array.shape)]
        where[longest] = (where[longest] + shift) % array.shape[longest]
        spots.append(tuple(where))
    return array.at[spots[0]].set(low).at[spots[1]].set(high)


def block_levels(rng, shape, pieces, least, high):
    def one(dim, shards_of):
        heights = jax.random.uniform(jax.random.fold_in(jax.random.fold_in(rng, 6), dim), (shards_of,), jnp.float32, least / len(pieces), high / len(pieces))
        return jnp.repeat(jnp.exp(heights), shape[dim] // shards_of).reshape((-1,) + (1,) * (len(shape) - dim - 1))

    gain = one(*pieces[0])
    for cut in pieces[1:]:
        gain = gain * one(*cut)
    return gain


def normal_values(own_key, dims, deviation, limit, cuts=(), kind=jnp.bfloat16):
    gain = block_levels(own_key, dims, cuts, -0.22, 0.18) if cuts else 1.0
    drawn = jax.random.normal(own_key, dims, jnp.float32) * deviation * gain
    return jnp.minimum(jnp.maximum(drawn, -limit), limit).astype(kind)


def setup_inputs(seed: int = 0, part: int = 0) -> dict:
    streams_of = jax.random.split(jax.random.key(seed), 5)
    own_keys = jax.random.split(jax.random.fold_in(streams_of[4], part), 5)
    return {
        "activations": normal_values(own_keys[0], (ROWS, DIN), 1.0, 6.0, ((0, 2), (1, 8))),
        "grads": draw_grads(jax.random.fold_in(jax.random.fold_in(streams_of[4], part), 71), part),
        "group_index": touch_ends(jax.random.randint(own_keys[2], (DOUT,), 0, GROUPS), jax.random.fold_in(own_keys[2], 1), 0, GROUPS - 1).astype(jnp.int32),
        "tile_list": draw_tile_list(jax.random.fold_in(streams_of[4], 71), part),
    }


def reference(activations, grads, group_index, tile_list):
    onehot = (group_index[:, None] == jnp.arange(GROUPS, dtype=jnp.int32)[None, :]).astype(jnp.float32)
    squares = grads.astype(jnp.float32) ** 2
    saliency = jnp.dot(squares, onehot, precision=lax.Precision.HIGHEST) * (GROUPS / DOUT)

    def one_slot(pair):
        row_block = pair[0]
        col_block = pair[1]
        live = (row_block >= 0).astype(jnp.float32)
        left = lax.dynamic_slice_in_dim(activations, (jnp.maximum(row_block, 0) * TILE).astype(jnp.int32), TILE, 1)
        right = lax.dynamic_slice_in_dim(activations, (jnp.maximum(col_block, 0) * TILE).astype(jnp.int32), TILE, 1)
        scaled = (left[:, None, :].astype(jnp.float32) * saliency[:, :, None]).astype(jnp.bfloat16)
        product = jnp.einsum("rkc,rb->ckb", scaled.astype(jnp.float32), right.astype(jnp.float32), precision=lax.Precision.HIGHEST)
        return product * (live / ROWS)

    tiles = lax.map(one_slot, tile_list)
    return jnp.transpose(tiles, (1, 0, 2, 3))
```

```python
import functools

import jax
import jax.numpy as jnp
import numpy as np
from jax import lax
from jax.experimental import pallas as pl
from jax.experimental.pallas import tpu as pltpu
from jax.sharding import PartitionSpec as P

GROUPS = 4
TILE = 256


def line_plan(positions):
    outward = [(2, 0), (3, 1), (4, 6), (5, 7)]
    inward = [(0, 2), (1, 3), (6, 4), (7, 5)]
    middle = [(2, 4), (3, 5), (4, 2), (5, 3)]
    outer_cross = [(0, 1), (1, 0), (6, 7), (7, 6)]
    inner_cross = [(2, 3), (3, 2), (4, 5), (5, 4)]
    sends = []

    def send(step, piece, pairs):
        sends.append((step, piece, pairs))
        return 1 + len(sends)

    out, mid, inn, outer, inner = {}, {}, {}, {}, {}
    for step, own in ((1, 0), (2, 1)):
        out[step] = send(step, own, outward)
        mid[step] = send(step, own, middle)
        inn[step] = send(step, own, inward)
        outer[step] = send(step, own, outer_cross)
        inner[step] = send(step, own, inner_cross)
    for step in range(3, 8):
        if step <= 6:
            out[step] = send(step, mid[step - 2], outward)
            inner[step] = send(step, mid[step - 2], inner_cross)
        else:
            inner[step] = send(step, inn[2], inner_cross)
            out[step] = send(step, inner[6], outward)
        outer[step] = send(step, out[step - 2], outer_cross)
        if step <= 4:
            mid[step] = send(step, inn[step - 2], middle)
        if step == 3:
            inn[step] = send(step, outer[1], inward)
    holds = [{0: (t, 0), 1: (t, 1)} for t in range(positions)]
    for number, (step, piece, pairs) in enumerate(sends):
        for source, target in pairs:
            holds[target][2 + number] = holds[source][piece]
    return sends, holds


def branch(index, low, high, action):
    if high - low == 1:
        action(low)
        return
    middle = (low + high) // 2

    @pl.when(index < middle)
    def _():
        branch(index, low, middle, action)

    @pl.when(index >= middle)
    def _():
        branch(index, middle, high, action)


def stage_kernel(tiles, table, place, saliency, *rest, pieces, stage, first, inverse, share):
    refs = rest[: 2 * pieces]
    rest = rest[2 * pieces :] if first else rest[2 * pieces + 1 :]
    out, left, right, result, zeros, todo, in_sem, out_sem, zero_sem = rest
    slots = tiles.shape[0]
    offset = place[0] * share

    def find(slot, count):
        row_ready = table[0, jnp.maximum(tiles[slot, 0], 0)]
        col_ready = table[0, jnp.maximum(tiles[slot, 1], 0)]
        live = tiles[slot, 0] >= 0
        mine = jnp.logical_and(live, jnp.maximum(row_ready, col_ready) == stage)

        @pl.when(mine)
        def _():
            todo[count] = slot

        return count + mine.astype(jnp.int32)

    total = lax.fori_loop(0, slots, find, jnp.int32(0))

    def load(position, buffer):
        row_block = tiles[todo[position], 0]
        col_block = tiles[todo[position], 1]
        left_at = pl.multiple_of(table[2, row_block] * TILE + offset, share)
        right_at = pl.multiple_of(table[2, col_block] * TILE, TILE)

        def start_left(piece):
            for side in range(2):
                pltpu.make_async_copy(
                    refs[2 * piece + side].at[:, pl.ds(left_at, share)],
                    left.at[buffer, side],
                    in_sem.at[buffer, side],
                ).start()

        def start_right(piece):
            for side in range(2):
                pltpu.make_async_copy(
                    refs[2 * piece + side].at[:, pl.ds(right_at, TILE)],
                    right.at[buffer, side],
                    in_sem.at[buffer, 2 + side],
                ).start()

        branch(table[1, row_block], 0, pieces, start_left)
        branch(table[1, col_block], 0, pieces, start_right)

    def wait_load(buffer):
        for side in range(2):
            for target, sem in ((left, side), (right, 2 + side)):
                there = target.at[buffer, side]
                pltpu.make_async_copy(there, there, in_sem.at[buffer, sem]).wait()

    def wait_store(buffer):
        there = result.at[buffer]
        pltpu.make_async_copy(there, there, out_sem.at[buffer]).wait()

    if first:
        zeros[...] = jnp.zeros_like(zeros)

        @pl.loop(0, slots)
        def _(slot):
            @pl.when(tiles[slot, 0] < 0)
            def _():
                pltpu.make_async_copy(zeros, out.at[:, slot], zero_sem).start()

    @pl.when(total > 0)
    def _():
        load(0, 0)

    @pl.loop(0, total)
    def _(position):
        buffer = position % 2

        @pl.when(position + 1 < total)
        def _():
            load(position + 1, 1 - buffer)

        wait_load(buffer)

        @pl.when(position >= 2)
        def _():
            wait_store(buffer)

        sums = [None] * GROUPS
        for side in range(2):
            turned = left[buffer, side].T.astype(jnp.float32)
            for group in range(GROUPS):
                scaled = (turned * saliency[side, group, :][None, :]).astype(jnp.bfloat16)
                product = jnp.dot(
                    scaled, right[buffer, side], preferred_element_type=jnp.float32
                )
                sums[group] = product if side == 0 else sums[group] + product
        for group in range(GROUPS):
            result[buffer, :, group, :] = sums[group] * inverse
        pltpu.make_async_copy(
            result.at[buffer], out.at[:, todo[position]], out_sem.at[buffer]
        ).start()

    for back in (2, 1):

        @pl.when(total >= back)
        def _():
            wait_store((total - back) % 2)

    if first:

        @pl.loop(0, slots)
        def _(slot):
            @pl.when(tiles[slot, 0] < 0)
            def _():
                pltpu.make_async_copy(zeros, zeros, zero_sem).wait()


def stage_call(tiles, table, place, saliency, refs, out, stage, inverse):
    first = out is None
    rows = refs[0].shape[0]
    slots = tiles.shape[0]
    share = TILE // 2
    scalar = pl.BlockSpec(memory_space=pltpu.SMEM)
    plain = pl.BlockSpec(memory_space=pl.ANY)
    pieces = len(refs) // 2
    tail = [] if first else [out]
    return pl.pallas_call(
        functools.partial(
            stage_kernel,
            pieces=pieces,
            stage=stage,
            first=first,
            inverse=inverse,
            share=share,
        ),
        out_shape=jax.ShapeDtypeStruct((share, slots, GROUPS, TILE), jnp.float32),
        in_specs=[scalar] * 3
        + [pl.BlockSpec(memory_space=pltpu.VMEM)]
        + [plain] * (len(refs) + len(tail)),
        out_specs=plain,
        scratch_shapes=[
            pltpu.VMEM((2, 2, rows, share), jnp.bfloat16),
            pltpu.VMEM((2, 2, rows, TILE), jnp.bfloat16),
            pltpu.VMEM((2, share, GROUPS, TILE), jnp.float32),
            pltpu.VMEM((share, GROUPS, TILE), jnp.float32),
            pltpu.SMEM((slots,), jnp.int32),
            pltpu.SemaphoreType.DMA((2, 4)),
            pltpu.SemaphoreType.DMA((2,)),
            pltpu.SemaphoreType.DMA,
        ],
        input_output_aliases={} if first else {4 + len(refs): 0},
        name=f"stage{stage}",
    )(tiles, table, place, saliency, *refs, *tail)


def group_saliency(grads, group_index, positions):
    onehot = (
        jnp.arange(GROUPS, dtype=jnp.int32)[:, None] == group_index[None, :]
    ).astype(jnp.float32)
    squares = grads.astype(jnp.float32) ** 2
    terms = lax.dot_general(
        onehot, squares, (((1,), (1,)), ((), ())), precision=lax.Precision.HIGHEST
    )
    total = terms
    for shift in range(1, positions):
        ring = [(t, (t + shift) % positions) for t in range(positions)]
        total = total + lax.ppermute(terms, "tile", ring)
    return total * (GROUPS / (grads.shape[1] * positions))


def swap(value):
    return lax.ppermute(value, "dp", [(0, 1), (1, 0)])


def body(activations, grads, group_index, tile_list):
    rows, columns = activations.shape
    positions = lax.axis_size("tile")
    blocks = columns * positions // TILE
    inverse = 1.0 / (rows * lax.axis_size("dp"))
    place = lax.axis_index("dp").astype(jnp.int32)[None]
    if positions == 8 and columns % (2 * TILE) == 0:
        saliency = group_saliency(grads, group_index, positions)
        saliency = jnp.stack([saliency, swap(saliency)])
        sends, holds = line_plan(positions)
        part = columns // 2
        stages = {0: 0, 1: 0, 2: 0, 3: 0, 4: 1, 5: 1, 6: 2, 7: 3}
        own = [activations[:, :part], activations[:, part:]]
        pieces = list(own)
        steps = [0, 0]
        others = [swap(own[0]), swap(own[1])]
        for step, piece, pairs in sends:
            pieces.append(lax.ppermute(pieces[piece], "tile", pairs))
            steps.append(step)
            joint = [(2 * t + d, 2 * t + 1 - d) for _, t in pairs for d in range(2)]
            others.append(lax.ppermute(pieces[-1], ("tile", "dp"), joint))
        table = np.zeros((positions, 3, blocks), np.int32)
        for t in range(positions):
            for piece, (source, which) in holds[t].items():
                for block in range(part // TILE):
                    at = (source * columns + which * part) // TILE + block
                    table[t, :, at] = (stages[steps[piece]], piece, block)
        table = jnp.asarray(table)[lax.axis_index("tile")]
        out = None
        for stage in range(4):
            count = sum(stages[s] <= stage for s in steps)
            refs = [r for pair in zip(pieces[:count], others[:count]) for r in pair]
            out = stage_call(tile_list, table, place, saliency, refs, out, stage, inverse)
        return out
    gathered = lax.all_gather(activations, "tile", axis=1, tiled=True)
    onehot = (
        jnp.arange(GROUPS, dtype=jnp.int32)[:, None] == group_index[None, :]
    ).astype(jnp.float32)
    squares = grads.astype(jnp.float32) ** 2
    terms = lax.dot_general(
        onehot, squares, (((1,), (1,)), ((), ())), precision=lax.Precision.HIGHEST
    )
    saliency = lax.psum(terms, "tile") * (GROUPS / (grads.shape[1] * positions))
    saliency = jnp.stack([saliency, swap(saliency)])
    where = np.zeros((3, blocks), np.int32)
    where[2] = np.arange(blocks)
    refs = [gathered, swap(gathered)]
    return stage_call(
        tile_list, jnp.asarray(where), place, saliency, refs, None, 0, inverse
    )


def solution(mesh):
    in_specs = (
        P(("groups", "dp"), "tile"),
        P(("groups", "dp"), "tile"),
        P(("groups", "tile")),
        P("tile", None),
    )
    out_specs = P("dp", ("groups", "tile"), None, None)
    return jax.shard_map(body, mesh=mesh, in_specs=in_specs, out_specs=out_specs, check_vma=False)
```
